1024 devices in a mesh: section: 16 (over y, x), expert: 64 (over z, core).
Axes of the slice: x: 4, y: 4, z: 32, core: 2. Of those that a mesh axis runs over, the one named last changes fastest.
Arguments:
- cotangent: bfloat16 [131072, 4096], P(('section', 'expert')), may hold values from -6 to 6
- expert_ids: int32 [131072, 1], P(('section', 'expert')), may hold values from 0 to 63; in each aligned block of 128 rows (0 to 127, 128 to 255, ...) at most 4 rows name the same one
- route_weight: float32 [131072], P(('section', 'expert')), may hold values from 0.1 to 1
- saved_preact: bfloat16 [131072, 2048], P(('section', 'expert')), may hold values from -6 to 6
- down_weight: bfloat16 [64, 1024, 4096], P('expert'), may hold values from -0.09375 to 0.09375
Outputs:
- d_preact: bfloat16 [131072, 2048], P(('section', 'expert'))
- d_route: float32 [131072], P(('section', 'expert'))
The draws below stay inside these ranges and needn't reach their ends.
Inputs may be any that keep to these rules, and one draw needn't show every extreme that they name: `expert_ids`: at most 4 of the 128 tokens of one device name the same expert, and on some devices one expert is named by exactly 4 of them.
All inputs are finite; a program needn't handle non-finite values.
Results may differ from the reference program's by a relative error of at most 0.0049.
Values may be sent and summed in bfloat16 or wider, within the bound.
No kernel may reach another device: no remote copies, remote signals or barrier semaphores. Data moves between devices by JAX's collectives and lax.ppermute only.
A program may use at most 32 MiB of HBM per device.

```python
import math
import jax
import jax.numpy as jnp
import numpy as np
from jax import lax

D = 4096
H = 1024
TOK_DEV = 128
EXPERTS = 64
CAP = 4
TOKENS = 131072
N_SECTION = 16
N_EXPERT = 64


def block_scale(key, dims, split, least, largest):
    def one(axis_at, blocks):
        steps = jax.random.uniform(jax.random.fold_in(jax.random.fold_in(key, 6), axis_at), (blocks,), jnp.float32, least / len(split), largest / len(split))
        return jnp.repeat(jnp.exp(steps), dims[axis_at] // blocks).reshape((-1,) + (1,) * (len(dims) - axis_at - 1))

    loudness = one(*split[0])
    for cut in split[1:]:
        loudness = loudness * one(*cut)
    return loudness


def shared_out(rng, own, number, rows, number_of, top, reach, lean):
    order = jax.random.permutation(rng, number_of)
    heavy_load, usual = load_shares(number_of, rows * top, reach, lean, True), load_shares(number_of, rows * top, reach, lean, False)
    places = jnp.arange(number_of)

    def named(sizes, turn):
        used = int((sizes > 0).sum())
        fixed = max(1, used // 4)
        moved = fixed + (places - fixed + turn * (used - fixed)) % max(1, number_of - fixed)
        return jnp.zeros((number_of,), jnp.int32).at[order[jnp.where(places < fixed, places, moved)]].set(jnp.asarray(sizes, jnp.int32))

    sizes = jnp.where(number % 4 == 0, named(heavy_load, number // 4), named(usual, number - number // 4 - 1))
    mixed = jax.random.permutation(jax.random.fold_in(own, 3), number_of)
    source_of, sink = mixed[0:number_of // 2 * 2:2], mixed[1:number_of // 2 * 2:2]
    room = jnp.minimum(sizes[source_of] - 1, reach - sizes[sink]) // 2
    room = jnp.where((source_of == order[0]) | (sink == order[0]) | (sizes[sink] == 0), 0, jnp.maximum(room, 0))
    moved = jax.random.randint(jax.random.fold_in(own, 4), (number_of // 2,), 0, 1 << 20) % (room + 1)
    sizes = sizes.at[source_of].add(-moved).at[sink].add(moved)
    members = jnp.searchsorted(jnp.cumsum(sizes), jnp.arange(rows * top), side="right").astype(jnp.int32)
    grid = members.reshape(top, rows).T
    grid = grid[jax.random.permutation(jax.random.fold_in(own, 1), rows)]
    turn = jax.random.randint(jax.random.fold_in(own, 2), (rows, 1), 0, top)
    return jnp.take_along_axis(grid, (jnp.arange(top)[None, :] + turn) % top, axis=1)


def load_shares(number_of, total, bound, slope, full):
    weights = [(1 << 20) // math.isqrt(rank ** slope) + 1 for rank in range(1, number_of + 1)]
    largest = bound if full else min(bound, max(-(-total // number_of), total * weights[0] // sum(weights)))
    least = 1 if total - largest >= number_of - 1 else 0
    given, surplus = [largest] + [least] * (number_of - 1), total - largest - least * (number_of - 1)
    while surplus > 0:
        movable = [i for i in range(1, number_of) if given[i] < largest] or [i for i in range(1, number_of) if given[i] < bound]
        whole, left = sum([weights[i] for i in movable]), surplus
        for i in movable:
            extra = min(bound - given[i], max(1, left * weights[i] // whole), surplus)
            given[i] = given[i] + extra
            surplus = surplus - extra
    return np.array(given)


def centred(key, dims, spread, bound, pieces=(), held_as=jnp.bfloat16):
    result = jax.random.normal(key, dims, jnp.float32) * spread
    if len(pieces) > 0:
        result = block_scale(key, dims, pieces, -0.22, 0.18) * result
    return jnp.clip(result, min=-bound, max=bound).astype(held_as)


def setup_inputs(seed: int = 0) -> dict:
    key_of = jax.random.split(jax.random.key(seed), 6)
    cotangent = centred(key_of[0], (TOKENS, D), 1.0, 6.0, ((0, 1024),))
    expert_ids_keys = jax.random.split(jax.random.fold_in(key_of[1], 1), TOKENS // TOK_DEV)
    expert_ids_turns = jax.random.permutation(jax.random.fold_in(key_of[1], 3), TOKENS // TOK_DEV)
    expert_ids = jax.vmap(lambda own, number: shared_out(jax.random.fold_in(key_of[1], 2), own, number, TOK_DEV, EXPERTS, 1, CAP, 2))(expert_ids_keys, expert_ids_turns).reshape((TOKENS, 1))
    route_weight = jnp.clip(0.1 + 0.9 * jax.random.uniform(key_of[2], (TOKENS,), jnp.float32) ** block_scale(key_of[2], (TOKENS,), ((0, 1024),), -0.2, 0.2), 0.1, 1.0)
    saved_preact = centred(key_of[3], (TOKENS, 2 * H), 1.5, 6.0, ((0, 1024),))
    down_weight = centred(key_of[4], (EXPERTS, H, D), D ** -0.5, 0.09375, ((0, 64),))
    return {"cotangent": cotangent, "expert_ids": expert_ids, "route_weight": route_weight, "saved_preact": saved_preact, "down_weight": down_weight}


def reference(cotangent, expert_ids, route_weight, saved_preact, down_weight):
    shifted_grad = jnp.roll(cotangent.reshape(N_SECTION, N_EXPERT * TOK_DEV, D), -1, axis=0)
    section_routes = expert_ids.reshape(N_SECTION, N_EXPERT * TOK_DEV).astype(jnp.int32)
    slot_depth = N_EXPERT * CAP

    def one_section(section_pair):
        row_data, route_index = section_pair
        onehot = (route_index[:, None] == jnp.arange(EXPERTS, dtype=jnp.int32)[None, :]).astype(jnp.int32)
        slot_rank = jnp.sum((jnp.cumsum(onehot, axis=0) - 1) * onehot, axis=1).astype(jnp.int32)
        flat_slot = (route_index * slot_depth + slot_rank).astype(jnp.int32)
        send_buffer = jnp.zeros((EXPERTS * slot_depth, D), row_data.dtype).at[flat_slot].set(row_data)
        send_buffer = send_buffer.reshape(EXPERTS, slot_depth, D)

        def one_expert(expert_pair):
            row_block, weight = expert_pair
            return jnp.dot(row_block, weight.T, preferred_element_type=jnp.float32).astype(jnp.bfloat16)

        products = lax.map(one_expert, (send_buffer, down_weight))
        return products.reshape(EXPERTS * slot_depth, H)[flat_slot]

    back_hidden = lax.map(one_section, (shifted_grad, section_routes)).reshape(TOKENS, H)
    gate_value = saved_preact[:, :H].astype(jnp.float32)
    up_value = saved_preact[:, H:].astype(jnp.float32)
    sigmoid_gate = jax.nn.sigmoid(gate_value)
    activated = gate_value * sigmoid_gate
    hidden = activated * up_value
    result_float = back_hidden.astype(jnp.float32)
    d_route = jnp.sum(result_float * hidden, axis=1)
    grad_hidden = route_weight[:, None] * result_float
    d_gate = grad_hidden * up_value * sigmoid_gate * (1.0 + gate_value * (1.0 - sigmoid_gate))
    d_up = grad_hidden * activated
    d_preact = jnp.concatenate([d_gate, d_up], axis=1).astype(jnp.bfloat16)
    return d_preact, d_route
```

```python
import jax
import jax.numpy as jnp
from jax import lax
from jax.sharding import PartitionSpec as P


SLOTS = 4
GROUP = 8


def moved(block, section_step, chip_step, flip=False, mirrored=False):
    sections, experts = lax.axis_size("section"), lax.axis_size("expert")
    chips = experts // 2
    route = []
    for source in range(sections * experts):
        section, place = divmod(source, experts)
        chip, core = divmod(place, 2)
        step = -chip_step if mirrored and core else chip_step
        target = ((chip + step) % chips) * 2 + (1 - core if flip else core)
        route.append((source, ((section + section_step) % sections) * experts + target))
    return lax.ppermute(block, ("section", "expert"), route)


def slots_of(expert, source, chip, core, chips):
    count = expert.shape[0]
    same = expert[:, None] == expert[None, :]
    earlier = jnp.arange(count)[None, :] < jnp.arange(count)[:, None]
    rank = jnp.sum((same & earlier).astype(jnp.int32), axis=1)
    distance = (expert // 2 - chip) % chips
    slot = distance * (2 * SLOTS) + source * SLOTS + rank
    return jnp.where(expert % 2 == core, slot, -1)


def local(cotangent, expert_ids, route_weight, saved_preact, down_weight):
    own = expert_ids[:, 0]
    weight = down_weight[0]
    width = weight.shape[0]
    experts = lax.axis_size("expert")
    chips = experts // 2
    place = lax.axis_index("expert")
    chip, core = place // 2, place % 2
    rows = chips * 2 * SLOTS

    partner_rows = moved(cotangent, 0, 0, flip=True)
    far_own = moved(own, 1, 0)
    far_partner = moved(own, 1, 0, flip=True)
    partner = moved(own, 0, 0, flip=True)

    far_slot = jnp.concatenate(
        [slots_of(far_own, 0, chip, core, chips), slots_of(far_partner, 1, chip, core, chips)]
    )
    pick = (jnp.arange(rows)[:, None] == far_slot[None, :]).astype(jnp.bfloat16)
    both = jnp.concatenate([cotangent, partner_rows], axis=0)
    send = jnp.dot(pick, both, preferred_element_type=jnp.float32).astype(jnp.bfloat16)

    half = chips // 2
    order = [half]
    for distance in range(half - 1, 0, -1):
        order += [distance, chips - distance]
    order += [0]

    def block(array, distance):
        return lax.slice_in_dim(array, distance * 2 * SLOTS, (distance + 1) * 2 * SLOTS)

    arrived = {}
    for distance in order:
        piece = block(send, distance)
        if distance == half:
            piece = moved(moved(piece, 0, half // 2, mirrored=True), 0, half // 2, mirrored=True)
        elif distance:
            piece = moved(piece, 0, distance if distance < half else distance - chips)
        arrived[distance] = piece

    returned = {}
    for first in range(0, chips, GROUP):
        members = order[first : first + GROUP]
        stacked = jnp.concatenate([arrived[d] for d in members], axis=0)
        dims = (((1,), (1,)), ((), ()))
        products = lax.dot_general(
            stacked, weight, dims, preferred_element_type=jnp.float32
        ).astype(jnp.bfloat16)
        for i, distance in enumerate(members):
            piece = block(products, i)
            if distance == half:
                piece = moved(piece, 0, half // 2, mirrored=True)
                piece = moved(piece, -1, half // 2, mirrored=True)
            else:
                piece = moved(piece, -1, -distance if distance < half else chips - distance)
            returned[distance] = piece
    result = jnp.concatenate([returned[d] for d in range(chips)], axis=0)

    def gathered(slot):
        take = (slot[:, None] == jnp.arange(rows)[None, :]).astype(jnp.bfloat16)
        return jnp.dot(take, result, preferred_element_type=jnp.float32)

    theirs = gathered(slots_of(partner, 1, chip, core, chips)).astype(jnp.bfloat16)
    mine = gathered(slots_of(own, 0, chip, core, chips))
    result_float = mine + moved(theirs, 0, 0, flip=True).astype(jnp.float32)

    gate_value = saved_preact[:, :width].astype(jnp.float32)
    up_value = saved_preact[:, width:].astype(jnp.float32)
    sigmoid_gate = jax.nn.sigmoid(gate_value)
    activated = gate_value * sigmoid_gate
    hidden = activated * up_value
    d_route = jnp.sum(result_float * hidden, axis=1)
    grad_hidden = route_weight[:, None] * result_float
    d_gate = grad_hidden * up_value * sigmoid_gate * (1.0 + gate_value * (1.0 - sigmoid_gate))
    d_up = grad_hidden * activated
    d_preact = jnp.concatenate([d_gate, d_up], axis=1).astype(jnp.bfloat16)
    return (d_preact, d_route)


def solution(mesh):
    in_specs = (
        P(("section", "expert"), None),
        P(("section", "expert"), None),
        P(("section", "expert")),
        P(("section", "expert"), None),
        P("expert", None, None),
    )
    out_specs = (P(("section", "expert"), None), P(("section", "expert")))
    return jax.shard_map(local, mesh=mesh, in_specs=in_specs, out_specs=out_specs, check_vma=False)
```

```python
import jax
import jax.numpy as jnp
from jax import lax
from jax.sharding import PartitionSpec as P

SLOTS = 2
ROUND = 16


def shifted(block, axis, distance):
    devices = range(lax.axis_size(axis))
    route = [((i - distance) % len(devices), i) for i in devices]
    return lax.ppermute(block, axis, route)


def expert_products(rows, weight):
    dims = (((1,), (1,)), ((), ()))
    return lax.dot_general(rows, weight, dims, preferred_element_type=jnp.float32).astype(
        jnp.bfloat16
    )


def onehot(left, right):
    return ((left[:, None] == right[None, :]) & (left[:, None] >= 0)).astype(jnp.bfloat16)


def pick(selection, rows):
    return jnp.dot(selection, rows, preferred_element_type=jnp.float32).astype(rows.dtype)


def count_before(flags):
    count = flags.shape[0]
    earlier = jnp.arange(count)[None, :] < jnp.arange(count)[:, None]
    return jnp.sum((flags[None, :] & earlier).astype(jnp.int32), axis=1)


def placed(expert):
    count = expert.shape[0]
    earlier = jnp.arange(count)[None, :] < jnp.arange(count)[:, None]
    same = expert[:, None] == expert[None, :]
    rank = jnp.sum((same & earlier).astype(jnp.int32), axis=1)
    beyond = rank >= SLOTS
    slot = jnp.where(beyond, -1, expert * SLOTS + rank)
    extra = jnp.where(beyond, count_before(beyond), -1)
    return slot, extra, jnp.sum(beyond.astype(jnp.int32))


def extra_round(turn, extra, expert, rows, weight):
    experts = lax.axis_size("expert")
    me = lax.axis_index("expert")
    turn_place = jnp.where(extra >= 0, extra - turn * ROUND, -1)
    selection = onehot(jnp.arange(ROUND, dtype=jnp.int32), turn_place)
    sent = pick(selection, rows)
    name = jnp.sum(selection * (expert + 1).astype(jnp.bfloat16)[None, :], axis=1, keepdims=True)
    sent = jnp.concatenate([sent, jnp.broadcast_to(name, (ROUND, 128))], axis=1)
    seen = lax.all_gather(sent, "expert", axis=0, tiled=True)
    width = rows.shape[1]
    mine = seen[:, width].astype(jnp.int32) == me + 1
    depth = experts * SLOTS
    order = jnp.where(mine, count_before(mine), -1)
    chosen = onehot(jnp.arange(depth, dtype=jnp.int32), order)
    products = expert_products(pick(chosen, seen[:, :width]), weight)
    spread = pick(onehot(order, jnp.arange(depth, dtype=jnp.int32)), products)
    back = lax.psum_scatter(spread, "expert", scatter_dimension=0, tiled=True)
    return pick(onehot(turn_place, jnp.arange(ROUND, dtype=jnp.int32)), back)


def local(cotangent, expert_ids, route_weight, saved_preact, down_weight):
    weight = down_weight[0]
    width = weight.shape[0]
    experts = lax.axis_size("expert")
    expert = shifted(expert_ids[:, 0], "section", 1)

    slot, extra, beyond = placed(expert)
    rounds = lax.pmax((beyond + ROUND - 1) // ROUND, ("section", "expert"))
    places = jnp.arange(experts * SLOTS, dtype=jnp.int32)

    first = extra_round(0, extra, expert, cotangent, weight)

    send = pick(onehot(places, slot), cotangent)
    received = lax.all_to_all(send, "expert", split_axis=0, concat_axis=0, tiled=True)
    products = expert_products(received, weight)
    returned = lax.all_to_all(products, "expert", split_axis=0, concat_axis=0, tiled=True)
    result = pick(onehot(slot, places), returned) + first

    def more(state):
        return state[0] < rounds

    def step(state):
        turn, total = state
        return turn + 1, total + extra_round(turn, extra, expert, cotangent, weight)

    result = lax.while_loop(more, step, (jnp.int32(1), result))[1]

    back_hidden = shifted(result, "section", -1)
    gate_value = saved_preact[:, :width].astype(jnp.float32)
    up_value = saved_preact[:, width:].astype(jnp.float32)
    sigmoid_gate = jax.nn.sigmoid(gate_value)
    activated = gate_value * sigmoid_gate
    hidden = activated * up_value
    result_float = back_hidden.astype(jnp.float32)
    d_route = jnp.sum(result_float * hidden, axis=1)
    grad_hidden = route_weight[:, None] * result_float
    d_gate = grad_hidden * up_value * sigmoid_gate * (1.0 + gate_value * (1.0 - sigmoid_gate))
    d_up = grad_hidden * activated
    d_preact = jnp.concatenate([d_gate, d_up], axis=1).astype(jnp.bfloat16)
    return (d_preact, d_route)


def solution(mesh):
    in_specs = (
        P(("section", "expert"), None),
        P(("section", "expert"), None),
        P(("section", "expert")),
        P(("section", "expert"), None),
        P("expert", None, None),
    )
    out_specs = (P(("section", "expert"), None), P(("section", "expert")))
    return jax.shard_map(local, mesh=mesh, in_specs=in_specs, out_specs=out_specs, check_vma=False)
```

```python
import jax
import jax.numpy as jnp
from jax import lax
from jax.sharding import PartitionSpec as P


SLOTS = 4
NEAR = 4
PAIR = 2 * SLOTS
CELL = 2 * PAIR
BLOCK = NEAR * CELL
PACKED = 48
NOTES = 128


def moved(block, section_step=0, chip_step=0, flip=False):
    experts = lax.axis_size("expert")
    chips = experts // 2

    def target(place):
        chip, core = divmod(place, 2)
        step = -chip_step if core else chip_step
        return ((chip + step) % chips) * 2 + (1 - core if flip else core)

    if not section_step:
        return lax.ppermute(block, "expert", [(i, target(i)) for i in range(experts)])
    sections = lax.axis_size("section")
    route = [
        (s * experts + i, ((s + section_step) % sections) * experts + target(i))
        for s in range(sections)
        for i in range(experts)
    ]
    return lax.ppermute(block, ("section", "expert"), route)


def numbers(count):
    return jnp.arange(count, dtype=jnp.int32)


def onehot(left, right):
    return (left[:, None] == right[None, :]).astype(jnp.bfloat16)


def picked(selection, rows):
    return jnp.dot(selection, rows, preferred_element_type=jnp.float32).astype(jnp.bfloat16)


def expert_products(rows, weight):
    dims = (((1,), (1,)), ((), ()))
    return lax.dot_general(rows, weight, dims, preferred_element_type=jnp.float32).astype(
        jnp.bfloat16
    )


def ranked(expert):
    place = numbers(expert.shape[0])
    same = (expert[:, None] == expert[None, :]) & (place[None, :] < place[:, None])
    return jnp.sum(same.astype(jnp.int32), axis=1)


def direct(rows, expert, rank, weight):
    experts = lax.axis_size("expert")
    slot = expert * SLOTS + rank
    places = numbers(experts * SLOTS)
    send = picked(onehot(places, slot), rows)
    received = lax.all_to_all(send, "expert", split_axis=0, concat_axis=0, tiled=True)
    products = expert_products(received, weight)
    returned = lax.all_to_all(products, "expert", split_axis=0, concat_axis=0, tiled=True)
    return picked(onehot(slot, places), returned)


def noted(rows, slot, flag):
    column = lax.broadcasted_iota(jnp.int32, (rows.shape[0], NOTES), 1)
    notes = jnp.where(column == 0, slot[:, None], jnp.where(column == 1, flag, 0))
    return jnp.concatenate([rows, notes.astype(jnp.bfloat16)], axis=1)


def packed(rows, far_rows, expert, far_expert, rank, weight):
    wide = rows.shape[1]
    experts = lax.axis_size("expert")
    chips = experts // 2
    half = chips // 2
    blocks = half // NEAR
    place = lax.axis_index("expert")
    chip, core = place // 2, place % 2
    tokens = expert.shape[0]

    both = jnp.concatenate([expert, far_expert])
    source = numbers(2 * tokens) // tokens
    inner = (both % 2) * SLOTS + jnp.concatenate([rank, ranked(far_expert)])
    ahead = (both // 2 - chip) % chips
    behind = (chip - both // 2) % chips

    def slots(distance, near):
        return jnp.where(near, distance * CELL + source * PAIR + inner, -1)

    forward = slots(ahead, ahead < half)
    backward = slots(behind, ahead > half)
    slot = jnp.where(core == 0, forward, backward)
    block = slot // BLOCK

    def fullest(which):
        return max_of(which // BLOCK)

    def max_of(index):
        hits = (index[None, :] == numbers(blocks)[1:, None]).astype(jnp.int32)
        return jnp.max(jnp.sum(hits, axis=1))

    flag = jnp.maximum(fullest(forward), fullest(backward)) > PACKED
    flag = flag.astype(jnp.int32)

    ahead_of = (block[:, None] == block[None, :]) & (slot[None, :] < slot[:, None])
    order = jnp.sum(ahead_of.astype(jnp.int32), axis=1)
    line = jnp.where(block == 0, slot, BLOCK + (block - 1) * PACKED + order)
    line = jnp.where((slot >= 0) & ((block == 0) | (order < PACKED)), line, -1)
    first = BLOCK + (blocks - 1) * PACKED
    opposite = (ahead == half) & (source == 0)
    line = jnp.where(opposite, first + inner, line)
    lines = numbers(first + PAIR)
    send_pick = onehot(lines, line)
    send = picked(send_pick, jnp.concatenate([rows, far_rows], axis=0))
    noted_slot = jnp.sum(
        jnp.where(lines[:, None] == line[None, :], slot[None, :] % BLOCK + 1, 0), axis=1
    )

    hold, hold_slot = [send[:BLOCK]], [numbers(BLOCK)]
    flags = flag
    spread = numbers(BLOCK)
    column = [(spread // CELL) * blocks * CELL + spread % CELL]
    for a in range(1, blocks):
        part = slice(BLOCK + (a - 1) * PACKED, BLOCK + a * PACKED)
        came = moved(noted(send[part], noted_slot[part], flag), chip_step=a * NEAR)
        hold.append(came[:, :wide])
        index = came[:, wide].astype(jnp.int32) - 1
        flags = jnp.maximum(flags, jnp.max(came[:, wide + 1].astype(jnp.int32)))
        column.append(
            jnp.where(index < 0, -1, (index // CELL) * blocks * CELL + a * CELL + index % CELL)
        )
    over = moved(noted(send[first:], numbers(PAIR), flag), chip_step=half)

    relay_pick = onehot(numbers(NEAR * blocks * CELL), jnp.concatenate(column))
    relay = picked(relay_pick, jnp.concatenate(hold, axis=0))
    step = blocks * CELL
    arrived = [relay[:step]]
    seen = jnp.maximum(flags, jnp.max(over[:, wide + 1].astype(jnp.int32)))
    for b in range(1, NEAR):
        piece = relay[b * step : (b + 1) * step]
        came = moved(noted(piece, numbers(step), flags), chip_step=b)
        arrived.append(came[:, :wide])
        seen = jnp.maximum(seen, jnp.max(came[:, wide + 1].astype(jnp.int32)))
    arrived.append(over[:, :wide])
    arrived = jnp.concatenate(arrived, axis=0)

    total = NEAR * step + PAIR
    part = total // 2
    spot = numbers(part)
    mine = (spot // SLOTS) * PAIR + core * SLOTS + spot % SLOTS
    theirs = (spot // SLOTS) * PAIR + (1 - core) * SLOTS + spot % SLOTS
    kept = picked(onehot(mine, numbers(total)), arrived)
    given = picked(onehot(theirs, numbers(total)), arrived)
    got = moved(noted(given, spot, seen), flip=True)
    seen = jnp.maximum(seen, jnp.max(got[:, wide + 1].astype(jnp.int32)))
    here = expert_products(jnp.concatenate([kept, got[:, :wide]], axis=0), weight)
    home = jnp.concatenate([here[:part], moved(here[part:], flip=True)], axis=0)
    back = picked(onehot(numbers(total), jnp.concatenate([mine, theirs])), home)

    relayed = [back[:step]]
    for b in range(1, NEAR):
        relayed.append(moved(back[b * step : (b + 1) * step], chip_step=-b))
    relayed = picked(relay_pick.T, jnp.concatenate(relayed, axis=0))
    final = [relayed[:BLOCK]]
    for a in range(1, blocks):
        piece = relayed[BLOCK + (a - 1) * PACKED : BLOCK + a * PACKED]
        final.append(moved(piece, chip_step=-a * NEAR))
    final.append(moved(back[NEAR * step :], chip_step=-half))
    final = jnp.concatenate(final, axis=0)
    own = picked(send_pick[:, :tokens].T, final)
    other = picked(send_pick[:, tokens:].T, final)
    return own + moved(other, flip=True), seen


def local(cotangent, expert_ids, route_weight, saved_preact, down_weight):
    weight = down_weight[0]
    width = weight.shape[0]
    far_rows = moved(cotangent, flip=True)
    expert = moved(expert_ids[:, 0], section_step=1)
    far_expert = moved(expert_ids[:, 0], section_step=1, flip=True)
    rank = ranked(expert)
    result, full = packed(cotangent, far_rows, expert, far_expert, rank, weight)
    result = lax.cond(
        full > 0,
        lambda: direct(cotangent, expert, rank, weight),
        lambda: result,
    )

    sections = lax.axis_size("section")
    route = [((i + 1) % sections, i) for i in range(sections)]
    back_hidden = lax.ppermute(result, "section", route)
    gate_value = saved_preact[:, :width].astype(jnp.float32)
    up_value = saved_preact[:, width:].astype(jnp.float32)
    sigmoid_gate = jax.nn.sigmoid(gate_value)
    activated = gate_value * sigmoid_gate
    hidden = activated * up_value
    result_float = back_hidden.astype(jnp.float32)
    d_route = jnp.sum(result_float * hidden, axis=1)
    grad_hidden = route_weight[:, None] * result_float
    d_gate = grad_hidden * up_value * sigmoid_gate * (1.0 + gate_value * (1.0 - sigmoid_gate))
    d_up = grad_hidden * activated
    d_preact = jnp.concatenate([d_gate, d_up], axis=1).astype(jnp.bfloat16)
    return (d_preact, d_route)


def solution(mesh):
    in_specs = (
        P(("section", "expert"), None),
        P(("section", "expert"), None),
        P(("section", "expert")),
        P(("section", "expert"), None),
        P("expert", None, None),
    )
    out_specs = (P(("section", "expert"), None), P(("section", "expert")))
    return jax.shard_map(local, mesh=mesh, in_specs=in_specs, out_specs=out_specs, check_vma=False)
```

```python
import jax
import jax.numpy as jnp
from jax import lax
from jax.sharding import PartitionSpec as P


SLOTS = 4
NEAR = 4
PAIR = 2 * SLOTS
CELL = 2 * PAIR
BLOCK = NEAR * CELL
PACKED = 48
NOTES = 128


def moved(block, section_step=0, chip_step=0, flip=False):
    experts = lax.axis_size("expert")
    chips = experts // 2

    def target(place):
        chip, core = divmod(place, 2)
        step = -chip_step if core else chip_step
        return ((chip + step) % chips) * 2 + (1 - core if flip else core)

    if not section_step:
        return lax.ppermute(block, "expert", [(i, target(i)) for i in range(experts)])
    sections = lax.axis_size("section")
    route = [
        (s * experts + i, ((s + section_step) % sections) * experts + target(i))
        for s in range(sections)
        for i in range(experts)
    ]
    return lax.ppermute(block, ("section", "expert"), route)


def numbers(count):
    return jnp.arange(count, dtype=jnp.int32)


def onehot(left, right):
    return (left[:, None] == right[None, :]).astype(jnp.bfloat16)


def picked(selection, rows):
    return jnp.dot(selection, rows, preferred_element_type=jnp.float32).astype(jnp.bfloat16)


def expert_products(rows, weight):
    dims = (((1,), (1,)), ((), ()))
    return lax.dot_general(rows, weight, dims, preferred_element_type=jnp.float32).astype(
        jnp.bfloat16
    )


def ranked(expert):
    place = numbers(expert.shape[0])
    same = (expert[:, None] == expert[None, :]) & (place[None, :] < place[:, None])
    return jnp.sum(same.astype(jnp.int32), axis=1)


def direct(rows, expert, rank, weight):
    experts = lax.axis_size("expert")
    slot = expert * SLOTS + rank
    places = numbers(experts * SLOTS)
    send = picked(onehot(places, slot), rows)
    received = lax.all_to_all(send, "expert", split_axis=0, concat_axis=0, tiled=True)
    products = expert_products(received, weight)
    returned = lax.all_to_all(products, "expert", split_axis=0, concat_axis=0, tiled=True)
    return picked(onehot(slot, places), returned)


def noted(rows, slot, flag):
    column = lax.broadcasted_iota(jnp.int32, (rows.shape[0], NOTES), 1)
    notes = jnp.where(column == 0, slot[:, None], jnp.where(column == 1, flag, 0))
    return jnp.concatenate([rows, notes.astype(jnp.bfloat16)], axis=1)


def packed(rows, far_rows, expert, far_expert, rank, weight):
    wide = rows.shape[1]
    experts = lax.axis_size("expert")
    chips = experts // 2
    half = chips // 2
    blocks = half // NEAR
    place = lax.axis_index("expert")
    chip, core = place // 2, place % 2
    tokens = expert.shape[0]

    both = jnp.concatenate([expert, far_expert])
    source = numbers(2 * tokens) // tokens
    ranks = jnp.concatenate([rank, ranked(far_expert)])
    crossing = (both + core) % 2
    ahead = (both // 2 - chip) % chips
    behind = (chip - both // 2) % chips
    forward = jnp.where(ahead < half, ahead, -1)
    backward = jnp.where(ahead > half, behind, -1)

    def fullest(distance):
        hits = (distance // NEAR)[None, :] == numbers(blocks)[1:, None]
        return jnp.max(jnp.sum(hits.astype(jnp.int32), axis=1))

    flag = (jnp.maximum(fullest(forward), fullest(backward)) > PACKED).astype(jnp.int32)

    distance = jnp.where(core == 0, forward, backward)
    block = distance // NEAR
    slot = distance * CELL + crossing * PAIR + source * SLOTS + ranks
    ahead_of = (block[:, None] == block[None, :]) & (slot[None, :] < slot[:, None])
    order = jnp.sum(ahead_of.astype(jnp.int32), axis=1)
    line = jnp.where(block == 0, slot, BLOCK + (block - 1) * PACKED + order)
    line = jnp.where((distance >= 0) & ((block == 0) | (order < PACKED)), line, -1)
    first = BLOCK + (blocks - 1) * PACKED
    opposite = (ahead == half) & (source == 0)
    line = jnp.where(opposite, first + crossing * SLOTS + ranks, line)
    lines = numbers(first + PAIR)
    send_pick = onehot(lines, line)
    send = picked(send_pick, jnp.concatenate([rows, far_rows], axis=0))
    noted_slot = jnp.sum(
        jnp.where(lines[:, None] == line[None, :], slot[None, :] % BLOCK + 1, 0), axis=1
    )

    def flag_in(block):
        return block[0, wide + 1].astype(jnp.int32)

    over = moved(noted(send[first:], numbers(PAIR), flag), chip_step=half)
    step = blocks * CELL

    def relay_row(index, a):
        side = (index // PAIR) % 2
        return (index // CELL) * step + side * (step // 2) + a * PAIR + index % PAIR

    hold = [noted(send[:BLOCK], numbers(BLOCK), flag)]
    flags = jnp.maximum(flag, flag_in(over))
    column = [relay_row(numbers(BLOCK), 0)]
    for a in range(1, blocks):
        part = slice(BLOCK + (a - 1) * PACKED, BLOCK + a * PACKED)
        came = moved(noted(send[part], noted_slot[part], flag), chip_step=a * NEAR)
        hold.append(came)
        index = came[:, wide].astype(jnp.int32) - 1
        flags = jnp.maximum(flags, flag_in(came))
        column.append(jnp.where(index < 0, -1, relay_row(index, a)))

    relay_pick = onehot(numbers(NEAR * step), jnp.concatenate(column))
    raised = jnp.where(numbers(wide + NOTES) == wide + 1, flags, 0).astype(jnp.float32)
    relay = jnp.dot(
        relay_pick, jnp.concatenate(hold, axis=0), preferred_element_type=jnp.float32
    )
    relay = (relay + raised[None, :]).astype(jnp.bfloat16)
    arrived = [relay[:step]]
    for b in range(1, NEAR):
        arrived.append(moved(relay[b * step : (b + 1) * step], chip_step=b))

    given = jnp.concatenate([p[step // 2 :] for p in arrived] + [over[SLOTS:]], axis=0)
    got = moved(given, flip=True)
    kept = jnp.concatenate([p[: step // 2] for p in arrived] + [over[:SLOTS]], axis=0)
    seen = jnp.maximum(jnp.max(kept[:, wide + 1]), jnp.max(got[:, wide + 1]))
    products = jnp.concatenate(
        [expert_products(kept[:, :wide], weight), expert_products(got[:, :wide], weight)], axis=0
    )

    spot = numbers(kept.shape[0])
    main = spot < NEAR * step // 2
    far = jnp.where(main, (spot % (step // 2)) // PAIR * NEAR + spot // (step // 2), half)
    other = jnp.where(main, (spot // SLOTS) % 2, 0)

    def target(lane):
        sign = 1 - 2 * lane
        return (((chip - sign * far) % chips) * 2 + (lane + other) % 2) * SLOTS + spot % SLOTS

    targets = jnp.concatenate([target(core), target(1 - core)])
    places = numbers(experts * SLOTS)
    returned = lax.all_to_all(
        picked(onehot(places, targets), products),
        "expert",
        split_axis=0,
        concat_axis=0,
        tiled=True,
    )
    return picked(onehot(expert * SLOTS + rank, places), returned), seen


def local(cotangent, expert_ids, route_weight, saved_preact, down_weight):
    weight = down_weight[0]
    width = weight.shape[0]
    far_rows = moved(cotangent, flip=True)
    expert = moved(expert_ids[:, 0], section_step=1)
    far_expert = moved(expert_ids[:, 0], section_step=1, flip=True)
    rank = ranked(expert)
    result, full = packed(cotangent, far_rows, expert, far_expert, rank, weight)
    result = lax.cond(
        full > 0,
        lambda: direct(cotangent, expert, rank, weight),
        lambda: result,
    )

    sections = lax.axis_size("section")
    route = [((i + 1) % sections, i) for i in range(sections)]
    back_hidden = lax.ppermute(result, "section", route)
    gate_value = saved_preact[:, :width].astype(jnp.float32)
    up_value = saved_preact[:, width:].astype(jnp.float32)
    sigmoid_gate = jax.nn.sigmoid(gate_value)
    activated = gate_value * sigmoid_gate
    hidden = activated * up_value
    result_float = back_hidden.astype(jnp.float32)
    d_route = jnp.sum(result_float * hidden, axis=1)
    grad_hidden = route_weight[:, None] * result_float
    d_gate = grad_hidden * up_value * sigmoid_gate * (1.0 + gate_value * (1.0 - sigmoid_gate))
    d_up = grad_hidden * activated
    d_preact = jnp.concatenate([d_gate, d_up], axis=1).astype(jnp.bfloat16)
    return (d_preact, d_route)


def solution(mesh):
    in_specs = (
        P(("section", "expert"), None),
        P(("section", "expert"), None),
        P(("section", "expert")),
        P(("section", "expert"), None),
        P("expert", None, None),
    )
    out_specs = (P(("section", "expert"), None), P(("section", "expert")))
    return jax.shard_map(local, mesh=mesh, in_specs=in_specs, out_specs=out_specs, check_vma=False)
```

```python
import jax
import jax.numpy as jnp
from jax import lax
from jax.sharding import PartitionSpec as P


SLOTS = 4
NEAR = 4
PAIR = 2 * SLOTS
CELL = 2 * PAIR
BLOCK = NEAR * CELL
PACKED = 48
PARTS = 2
NOTES = 128


def moved(block, section_step=0, chip_step=0, flip=False):
    experts = lax.axis_size("expert")
    chips = experts // 2

    def target(place):
        chip, core = divmod(place, 2)
        step = -chip_step if core else chip_step
        return ((chip + step) % chips) * 2 + (1 - core if flip else core)

    if not section_step:
        return lax.ppermute(block, "expert", [(i, target(i)) for i in range(experts)])
    sections = lax.axis_size("section")
    route = [
        (s * experts + i, ((s + section_step) % sections) * experts + target(i))
        for s in range(sections)
        for i in range(experts)
    ]
    return lax.ppermute(block, ("section", "expert"), route)


def numbers(count):
    return jnp.arange(count, dtype=jnp.int32)


def onehot(left, right):
    return (left[:, None] == right[None, :]).astype(jnp.bfloat16)


def picked(selection, rows):
    return jnp.dot(selection, rows, preferred_element_type=jnp.float32).astype(jnp.bfloat16)


def expert_products(rows, weight):
    dims = (((1,), (1,)), ((), ()))
    return lax.dot_general(rows, weight, dims, preferred_element_type=jnp.float32).astype(
        jnp.bfloat16
    )


def ranked(expert):
    place = numbers(expert.shape[0])
    same = (expert[:, None] == expert[None, :]) & (place[None, :] < place[:, None])
    return jnp.sum(same.astype(jnp.int32), axis=1)


def direct(rows, expert, rank, weight):
    experts = lax.axis_size("expert")
    slot = expert * SLOTS + rank
    places = numbers(experts * SLOTS)
    send = picked(onehot(places, slot), rows)
    received = lax.all_to_all(send, "expert", split_axis=0, concat_axis=0, tiled=True)
    products = expert_products(received, weight)
    returned = lax.all_to_all(products, "expert", split_axis=0, concat_axis=0, tiled=True)
    return picked(onehot(slot, places), returned)


def noted(rows, slot, flag):
    column = lax.broadcasted_iota(jnp.int32, (rows.shape[0], NOTES), 1)
    notes = jnp.where(column == 0, slot[:, None], jnp.where(column == 1, flag, 0))
    return jnp.concatenate([rows, notes.astype(jnp.bfloat16)], axis=1)


def packed(rows, far_rows, expert, far_expert, rank, weight):
    wide = rows.shape[1]
    experts = lax.axis_size("expert")
    chips = experts // 2
    half = chips // 2
    blocks = half // NEAR
    place = lax.axis_index("expert")
    chip, core = place // 2, place % 2
    tokens = expert.shape[0]

    both = jnp.concatenate([expert, far_expert])
    source = numbers(2 * tokens) // tokens
    ranks = jnp.concatenate([rank, ranked(far_expert)])
    crossing = (both + core) % 2
    ahead = (both // 2 - chip) % chips
    behind = (chip - both // 2) % chips
    forward = jnp.where(ahead < half, ahead, -1)
    backward = jnp.where(ahead > half, behind, -1)

    way = jnp.where(backward > 0, blocks + backward // NEAR, forward // NEAR)
    hits = (way[None, :] == numbers(2 * blocks)[:, None]) & (way % blocks > 0)[None, :]
    flag = (jnp.max(jnp.sum(hits.astype(jnp.int32), axis=1)) > PACKED).astype(jnp.int32)

    distance = jnp.where(core == 0, forward, backward)
    block = distance // NEAR
    slot = distance * CELL + crossing * PAIR + source * SLOTS + ranks
    ahead_of = (block[:, None] == block[None, :]) & (slot[None, :] < slot[:, None])
    order = jnp.sum(ahead_of.astype(jnp.int32), axis=1)
    line = jnp.where(block == 0, slot, BLOCK + (block - 1) * PACKED + order)
    line = jnp.where((distance >= 0) & ((block == 0) | (order < PACKED)), line, -1)
    first = BLOCK + (blocks - 1) * PACKED
    opposite = (ahead == half) & (source == 0)
    line = jnp.where(opposite, first + crossing * SLOTS + ranks, line)
    lines = numbers(first + PAIR)
    send_pick = onehot(lines, line)
    noted_slot = jnp.sum(
        jnp.where(lines[:, None] == line[None, :], slot[None, :] % BLOCK + 1, 0), axis=1
    )
    step = blocks * CELL
    side = step // 2

    def relay_row(index, a):
        across = (index // PAIR) % 2
        return (index // CELL) * step + across * side + a * PAIR + index % PAIR

    def flag_in(block):
        return block[0, cut + 1].astype(jnp.int32)

    cut = wide // PARTS
    shares = [slice(h * cut, (h + 1) * cut) for h in range(PARTS)]
    sends, first_leg = [], []
    for h, share in enumerate(shares):
        both_rows = jnp.concatenate([rows[:, share], far_rows[:, share]], axis=0)
        send = picked(send_pick, both_rows)
        sends.append(send)
        came = []
        for a in range(1, blocks):
            part = slice(BLOCK + (a - 1) * PACKED, BLOCK + a * PACKED)
            piece = noted(send[part], noted_slot[part], flag) if h == 0 else send[part]
            came.append(moved(piece, chip_step=a * NEAR))
        first_leg.append(came)
    last = jnp.concatenate([noted(sends[0][first:], numbers(PAIR), flag)]
                           + [send[first:] for send in sends[1:]], axis=1)
    last = moved(last, chip_step=half)
    over = [last[:, : cut + NOTES]]
    over += [last[:, h * cut + NOTES : (h + 1) * cut + NOTES] for h in range(1, PARTS)]

    flags = jnp.maximum(flag, flag_in(over[0]))
    column = [relay_row(numbers(BLOCK), 0)]
    for a, came in enumerate(first_leg[0], 1):
        index = came[:, cut].astype(jnp.int32) - 1
        flags = jnp.maximum(flags, flag_in(came))
        column.append(jnp.where(index < 0, -1, relay_row(index, a)))
    relay_pick = onehot(numbers(NEAR * step), jnp.concatenate(column))
    raised = jnp.where(numbers(cut + NOTES) == cut + 1, flags, 0).astype(jnp.float32)

    products, seen, previous = 0.0, None, []
    for h, share in enumerate(shares):
        own = sends[h][:BLOCK]
        own = noted(own, numbers(BLOCK), flag) if h == 0 else own
        came = first_leg[h]
        if h:
            came, previous = lax.optimization_barrier((came, previous))
        hold = jnp.concatenate([own] + came, axis=0)
        relay = jnp.dot(relay_pick, hold, preferred_element_type=jnp.float32)
        relay = ((relay + raised[None, :]) if h == 0 else relay).astype(jnp.bfloat16)
        arrived = [relay[:step]]
        for b in range(1, NEAR):
            arrived.append(moved(relay[b * step : (b + 1) * step], chip_step=b))
        previous = arrived[1:]
        if h:
            arrived, products = lax.optimization_barrier((arrived, products))
        given = jnp.concatenate([p[side:] for p in arrived] + [over[h][SLOTS:]], axis=0)
        kept = jnp.concatenate([p[:side] for p in arrived] + [over[h][:SLOTS]], axis=0)
        got = moved(given, flip=True)
        if h == 0:
            seen = jnp.maximum(jnp.max(kept[:, cut + 1]), jnp.max(got[:, cut + 1]))
        met = jnp.concatenate([kept[:, :cut], got[:, :cut]], axis=0)
        dims = (((1,), (1,)), ((), ()))
        products += lax.dot_general(
            met, weight[:, share], dims, preferred_element_type=jnp.float32
        )
    products = products.astype(jnp.bfloat16)

    spot = numbers(kept.shape[0])
    main = spot < NEAR * step // 2
    far = jnp.where(main, (spot % (step // 2)) // PAIR * NEAR + spot // (step // 2), half)
    other = jnp.where(main, (spot // SLOTS) % 2, 0)

    def target(lane):
        sign = 1 - 2 * lane
        return (((chip - sign * far) % chips) * 2 + (lane + other) % 2) * SLOTS + spot % SLOTS

    targets = jnp.concatenate([target(core), target(1 - core)])
    places = numbers(experts * SLOTS)
    returned = lax.all_to_all(
        picked(onehot(places, targets), products),
        "expert",
        split_axis=0,
        concat_axis=0,
        tiled=True,
    )
    return picked(onehot(expert * SLOTS + rank, places), returned), seen


def local(cotangent, expert_ids, route_weight, saved_preact, down_weight):
    weight = down_weight[0]
    width = weight.shape[0]
    far_rows = moved(cotangent, flip=True)
    expert = moved(expert_ids[:, 0], section_step=1)
    far_expert = moved(expert_ids[:, 0], section_step=1, flip=True)
    rank = ranked(expert)
    result, full = packed(cotangent, far_rows, expert, far_expert, rank, weight)
    result = lax.cond(
        full > 0,
        lambda: direct(cotangent, expert, rank, weight),
        lambda: result,
    )

    sections = lax.axis_size("section")
    route = [((i + 1) % sections, i) for i in range(sections)]
    back_hidden = lax.ppermute(result, "section", route)
    gate_value = saved_preact[:, :width].astype(jnp.float32)
    up_value = saved_preact[:, width:].astype(jnp.float32)
    sigmoid_gate = jax.nn.sigmoid(gate_value)
    activated = gate_value * sigmoid_gate
    hidden = activated * up_value
    result_float = back_hidden.astype(jnp.float32)
    d_route = jnp.sum(result_float * hidden, axis=1)
    grad_hidden = route_weight[:, None] * result_float
    d_gate = grad_hidden * up_value * sigmoid_gate * (1.0 + gate_value * (1.0 - sigmoid_gate))
    d_up = grad_hidden * activated
    d_preact = jnp.concatenate([d_gate, d_up], axis=1).astype(jnp.bfloat16)
    return (d_preact, d_route)


def solution(mesh):
    in_specs = (
        P(("section", "expert"), None),
        P(("section", "expert"), None),
        P(("section", "expert")),
        P(("section", "expert"), None),
        P("expert", None, None),
    )
    out_specs = (P(("section", "expert"), None), P(("section", "expert")))
    return jax.shard_map(local, mesh=mesh, in_specs=in_specs, out_specs=out_specs, check_vma=False)
```

```python
import jax
import jax.numpy as jnp
from jax import lax
from jax.sharding import PartitionSpec as P


SLOTS = 4
NEAR = 4
PAIR = 2 * SLOTS
CELL = 2 * PAIR
BLOCK = NEAR * CELL
PACKED = 48
PARTS = 2
NOTES = 128


def moved(block, section_step=0, chip_step=0, flip=False):
    experts = lax.axis_size("expert")
    chips = experts // 2

    def target(place):
        chip, core = divmod(place, 2)
        step = -chip_step if core else chip_step
        return ((chip + step) % chips) * 2 + (1 - core if flip else core)

    if not section_step:
        return lax.ppermute(block, "expert", [(i, target(i)) for i in range(experts)])
    sections = lax.axis_size("section")
    route = [
        (s * experts + i, ((s + section_step) % sections) * experts + target(i))
        for s in range(sections)
        for i in range(experts)
    ]
    return lax.ppermute(block, ("section", "expert"), route)


def numbers(count):
    return jnp.arange(count, dtype=jnp.int32)


def onehot(left, right):
    return (left[:, None] == right[None, :]).astype(jnp.bfloat16)


def picked(selection, rows):
    return jnp.dot(selection, rows, preferred_element_type=jnp.float32).astype(jnp.bfloat16)


def expert_products(rows, weight):
    dims = (((1,), (1,)), ((), ()))
    return lax.dot_general(rows, weight, dims, preferred_element_type=jnp.float32).astype(
        jnp.bfloat16
    )


def ranked(expert):
    place = numbers(expert.shape[0])
    same = (expert[:, None] == expert[None, :]) & (place[None, :] < place[:, None])
    return jnp.sum(same.astype(jnp.int32), axis=1)


def direct(rows, expert, rank, weight):
    experts = lax.axis_size("expert")
    slot = expert * SLOTS + rank
    places = numbers(experts * SLOTS)
    send = picked(onehot(places, slot), rows)
    received = lax.all_to_all(send, "expert", split_axis=0, concat_axis=0, tiled=True)
    products = expert_products(received, weight)
    returned = lax.all_to_all(products, "expert", split_axis=0, concat_axis=0, tiled=True)
    return picked(onehot(slot, places), returned)


def noted(rows, slot, flag):
    column = lax.broadcasted_iota(jnp.int32, (rows.shape[0], NOTES), 1)
    notes = jnp.where(column == 0, slot[:, None], jnp.where(column == 1, flag, 0))
    return jnp.concatenate([rows, notes.astype(jnp.bfloat16)], axis=1)


def packed(rows, far_rows, expert, far_expert, rank, weight):
    wide = rows.shape[1]
    experts = lax.axis_size("expert")
    chips = experts // 2
    half = chips // 2
    blocks = half // NEAR
    place = lax.axis_index("expert")
    chip, core = place // 2, place % 2
    tokens = expert.shape[0]

    both = jnp.concatenate([expert, far_expert])
    source = numbers(2 * tokens) // tokens
    ranks = jnp.concatenate([rank, ranked(far_expert)])
    crossing = (both + core) % 2
    ahead = (both // 2 - chip) % chips
    behind = (chip - both // 2) % chips
    forward = jnp.where(ahead < half, ahead, -1)
    backward = jnp.where(ahead > half, behind, -1)

    way = jnp.where(backward > 0, blocks + backward // NEAR, forward // NEAR)
    hits = (way[None, :] == numbers(2 * blocks)[:, None]) & (way % blocks > 0)[None, :]
    flag = (jnp.max(jnp.sum(hits.astype(jnp.int32), axis=1)) > PACKED).astype(jnp.int32)

    distance = jnp.where(core == 0, forward, backward)
    block = distance // NEAR
    slot = distance * CELL + crossing * PAIR + source * SLOTS + ranks
    ahead_of = (block[:, None] == block[None, :]) & (slot[None, :] < slot[:, None])
    order = jnp.sum(ahead_of.astype(jnp.int32), axis=1)
    line = jnp.where(block == 0, slot, BLOCK + (block - 1) * PACKED + order)
    line = jnp.where((distance >= 0) & ((block == 0) | (order < PACKED)), line, -1)
    first = BLOCK + (blocks - 1) * PACKED
    opposite = (ahead == half) & (source == 0)
    line = jnp.where(opposite, first + crossing * SLOTS + ranks, line)
    lines = numbers(first + PAIR)
    send_pick = onehot(lines, line)
    noted_slot = jnp.sum(
        jnp.where(lines[:, None] == line[None, :], slot[None, :] % BLOCK + 1, 0), axis=1
    )
    step = blocks * CELL
    side = step // 2

    def relay_row(index, a):
        across = (index // PAIR) % 2
        return (index // CELL) * step + across * side + a * PAIR + index % PAIR

    cut = wide // PARTS
    shares = [slice(h * cut, (h + 1) * cut) for h in range(PARTS)]
    sends, first_leg = [], []
    for h, share in enumerate(shares):
        both_rows = jnp.concatenate([rows[:, share], far_rows[:, share]], axis=0)
        send = picked(send_pick, both_rows)
        sends.append(send)
        came = []
        for a in range(1, blocks):
            part = slice(BLOCK + (a - 1) * PACKED, BLOCK + a * PACKED)
            piece = noted(send[part], noted_slot[part], flag) if h == 0 else send[part]
            came.append(moved(piece, chip_step=a * NEAR))
        first_leg.append(came)
    last = jnp.concatenate([noted(sends[0][first:], numbers(PAIR), flag)]
                           + [send[first:] for send in sends[1:]], axis=1)
    last = moved(last, chip_step=half)
    over = [last[:, : cut + NOTES]]
    over += [last[:, h * cut + NOTES : (h + 1) * cut + NOTES] for h in range(1, PARTS)]

    column = [relay_row(numbers(BLOCK), 0)]
    for a, came in enumerate(first_leg[0], 1):
        index = came[:, cut].astype(jnp.int32) - 1
        column.append(jnp.where(index < 0, -1, relay_row(index, a)))
    relay_pick = onehot(numbers(NEAR * step), jnp.concatenate(column))

    products, seen, previous = 0.0, None, []
    for h, share in enumerate(shares):
        own = sends[h][:BLOCK]
        own = noted(own, numbers(BLOCK), flag) if h == 0 else own
        came = first_leg[h]
        if h:
            came, previous = lax.optimization_barrier((came, previous))
        hold = jnp.concatenate([own] + came, axis=0)
        relay = jnp.dot(relay_pick, hold, preferred_element_type=jnp.float32)
        if h == 0:
            notes = jnp.sum(hold[:, cut:].astype(jnp.float32), axis=0)
            raised = jnp.where(numbers(NOTES) == 1, jnp.minimum(notes, 1.0), 0.0)
            relay = relay + jnp.pad(raised, (cut, 0))[None, :]
        relay = relay.astype(jnp.bfloat16)
        arrived = [relay[:step]]
        for b in range(1, NEAR):
            arrived.append(moved(relay[b * step : (b + 1) * step], chip_step=b))
        previous = arrived[1:]
        if h:
            arrived, products = lax.optimization_barrier((arrived, products))
        given = jnp.concatenate([p[side:] for p in arrived] + [over[h][SLOTS:]], axis=0)
        kept = jnp.concatenate([p[:side] for p in arrived] + [over[h][:SLOTS]], axis=0)
        got = moved(given, flip=True)
        if h == 0:
            seen = jnp.maximum(jnp.max(kept[:, cut + 1]), jnp.max(got[:, cut + 1]))
        met = jnp.concatenate([kept[:, :cut], got[:, :cut]], axis=0)
        dims = (((1,), (1,)), ((), ()))
        products += lax.dot_general(
            met, weight[:, share], dims, preferred_element_type=jnp.float32
        )
    products = products.astype(jnp.bfloat16)

    spot = numbers(kept.shape[0])
    main = spot < NEAR * step // 2
    far = jnp.where(main, (spot % (step // 2)) // PAIR * NEAR + spot // (step // 2), half)
    other = jnp.where(main, (spot // SLOTS) % 2, 0)

    def target(lane):
        sign = 1 - 2 * lane
        return (((chip - sign * far) % chips) * 2 + (lane + other) % 2) * SLOTS + spot % SLOTS

    targets = jnp.concatenate([target(core), target(1 - core)])
    places = numbers(experts * SLOTS)
    returned = lax.all_to_all(
        picked(onehot(places, targets), products),
        "expert",
        split_axis=0,
        concat_axis=0,
        tiled=True,
    )
    return picked(onehot(expert * SLOTS + rank, places), returned), seen


def local(cotangent, expert_ids, route_weight, saved_preact, down_weight):
    weight = down_weight[0]
    width = weight.shape[0]
    far_rows = moved(cotangent, flip=True)
    expert = moved(expert_ids[:, 0], section_step=1)
    far_expert = moved(expert_ids[:, 0], section_step=1, flip=True)
    rank = ranked(expert)
    result, full = packed(cotangent, far_rows, expert, far_expert, rank, weight)
    result = lax.cond(
        full > 0,
        lambda: direct(cotangent, expert, rank, weight),
        lambda: result,
    )

    sections = lax.axis_size("section")
    route = [((i + 1) % sections, i) for i in range(sections)]
    back_hidden = lax.ppermute(result, "section", route)
    gate_value = saved_preact[:, :width].astype(jnp.float32)
    up_value = saved_preact[:, width:].astype(jnp.float32)
    sigmoid_gate = jax.nn.sigmoid(gate_value)
    activated = gate_value * sigmoid_gate
    hidden = activated * up_value
    result_float = back_hidden.astype(jnp.float32)
    d_route = jnp.sum(result_float * hidden, axis=1)
    grad_hidden = route_weight[:, None] * result_float
    d_gate = grad_hidden * up_value * sigmoid_gate * (1.0 + gate_value * (1.0 - sigmoid_gate))
    d_up = grad_hidden * activated
    d_preact = jnp.concatenate([d_gate, d_up], axis=1).astype(jnp.bfloat16)
    return (d_preact, d_route)


def solution(mesh):
    in_specs = (
        P(("section", "expert"), None),
        P(("section", "expert"), None),
        P(("section", "expert")),
        P(("section", "expert"), None),
        P("expert", None, None),
    )
    out_specs = (P(("section", "expert"), None), P(("section", "expert")))
    return jax.shard_map(local, mesh=mesh, in_specs=in_specs, out_specs=out_specs, check_vma=False)
```

```python
import jax
import jax.numpy as jnp
from jax import lax
from jax.sharding import PartitionSpec as P


SLOTS = 4
NEAR = 4
PAIR = 2 * SLOTS
CELL = 2 * PAIR
BLOCK = NEAR * CELL
PACKED = 48
PARTS = 2
NOTES = 128


def moved(block, section_step=0, chip_step=0, flip=False):
    experts = lax.axis_size("expert")
    chips = experts // 2

    def target(place):
        chip, core = divmod(place, 2)
        step = -chip_step if core else chip_step
        return ((chip + step) % chips) * 2 + (1 - core if flip else core)

    if not section_step:
        return lax.ppermute(block, "expert", [(i, target(i)) for i in range(experts)])
    sections = lax.axis_size("section")
    route = [
        (s * experts + i, ((s + section_step) % sections) * experts + target(i))
        for s in range(sections)
        for i in range(experts)
    ]
    return lax.ppermute(block, ("section", "expert"), route)


def numbers(count):
    return jnp.arange(count, dtype=jnp.int32)


def onehot(left, right):
    return (left[:, None] == right[None, :]).astype(jnp.bfloat16)


def picked(selection, rows):
    return jnp.dot(selection, rows, preferred_element_type=jnp.float32).astype(jnp.bfloat16)


def expert_products(rows, weight):
    dims = (((1,), (1,)), ((), ()))
    return lax.dot_general(rows, weight, dims, preferred_element_type=jnp.float32).astype(
        jnp.bfloat16
    )


def ranked(expert):
    place = numbers(expert.shape[0])
    same = (expert[:, None] == expert[None, :]) & (place[None, :] < place[:, None])
    return jnp.sum(same.astype(jnp.int32), axis=1)


def direct(rows, expert, rank, weight):
    experts = lax.axis_size("expert")
    slot = expert * SLOTS + rank
    places = numbers(experts * SLOTS)
    send = picked(onehot(places, slot), rows)
    received = lax.all_to_all(send, "expert", split_axis=0, concat_axis=0, tiled=True)
    products = expert_products(received, weight)
    returned = lax.all_to_all(products, "expert", split_axis=0, concat_axis=0, tiled=True)
    return picked(onehot(slot, places), returned)


def noted(rows, slot, flag):
    column = lax.broadcasted_iota(jnp.int32, (rows.shape[0], NOTES), 1)
    notes = jnp.where(column == 0, slot[:, None], jnp.where(column == 1, flag, 0))
    return jnp.concatenate([rows, notes.astype(jnp.bfloat16)], axis=1)


def packed(rows, far_rows, expert, far_expert, rank, weight):
    wide = rows.shape[1]
    experts = lax.axis_size("expert")
    chips = experts // 2
    half = chips // 2
    blocks = half // NEAR
    place = lax.axis_index("expert")
    chip, core = place // 2, place % 2
    tokens = expert.shape[0]

    both = jnp.concatenate([expert, far_expert])
    source = numbers(2 * tokens) // tokens
    ranks = jnp.concatenate([rank, ranked(far_expert)])
    crossing = (both + core) % 2
    ahead = (both // 2 - chip) % chips
    behind = (chip - both // 2) % chips
    forward = jnp.where(ahead < half, ahead, -1)
    backward = jnp.where(ahead > half, behind, -1)

    way = jnp.where(backward > 0, blocks + backward // NEAR, forward // NEAR)
    hits = (way[None, :] == numbers(2 * blocks)[:, None]) & (way % blocks > 0)[None, :]
    flag = (jnp.max(jnp.sum(hits.astype(jnp.int32), axis=1)) > PACKED).astype(jnp.int32)

    distance = jnp.where(core == 0, forward, backward)
    block = distance // NEAR
    slot = distance * CELL + crossing * PAIR + source * SLOTS + ranks
    ahead_of = (block[:, None] == block[None, :]) & (slot[None, :] < slot[:, None])
    order = jnp.sum(ahead_of.astype(jnp.int32), axis=1)
    line = jnp.where(block == 0, slot, BLOCK + (block - 1) * PACKED + order)
    line = jnp.where((distance >= 0) & ((block == 0) | (order < PACKED)), line, -1)
    first = BLOCK + (blocks - 1) * PACKED
    opposite = (ahead == half) & (source == 0)
    line = jnp.where(opposite, first + crossing * SLOTS + ranks, line)
    lines = numbers(first + PAIR)
    send_pick = onehot(lines, line)
    noted_slot = jnp.sum(
        jnp.where(lines[:, None] == line[None, :], slot[None, :] % BLOCK + 1, 0), axis=1
    )
    step = blocks * CELL
    side = step // 2

    def relay_row(index, a):
        across = (index // PAIR) % 2
        return (index // CELL) * step + across * side + a * PAIR + index % PAIR

    cut = wide // PARTS
    shares = [slice(h * cut, (h + 1) * cut) for h in range(PARTS)]
    sends, first_leg = [], []
    for h, share in enumerate(shares):
        both_rows = jnp.concatenate([rows[:, share], far_rows[:, share]], axis=0)
        send = picked(send_pick, both_rows)
        sends.append(send)
        came = []
        for a in range(1, blocks):
            part = slice(BLOCK + (a - 1) * PACKED, BLOCK + a * PACKED)
            piece = noted(send[part], noted_slot[part], flag) if h == 0 else send[part]
            came.append(moved(piece, chip_step=a * NEAR))
        first_leg.append(came)
    last = jnp.concatenate([noted(sends[0][first:], numbers(PAIR), flag)]
                           + [send[first:] for send in sends[1:]], axis=1)
    last = moved(last, chip_step=half)
    over = [last[:, : cut + NOTES]]
    over += [last[:, h * cut + NOTES : (h + 1) * cut + NOTES] for h in range(1, PARTS)]

    column = [relay_row(numbers(BLOCK), 0)]
    for a, came in enumerate(first_leg[0], 1):
        index = came[:, cut].astype(jnp.int32) - 1
        column.append(jnp.where(index < 0, -1, relay_row(index, a)))
    relay_pick = onehot(numbers(NEAR * step), jnp.concatenate(column))

    products, seen, previous = 0.0, None, []
    for h, share in enumerate(shares):
        own = sends[h][:BLOCK]
        own = noted(own, numbers(BLOCK), flag) if h == 0 else own
        came = first_leg[h]
        if h:
            came, previous = lax.optimization_barrier((came, previous))
        hold = jnp.concatenate([own] + came, axis=0)
        relay = jnp.dot(relay_pick, hold, preferred_element_type=jnp.float32)
        if h == 0:
            notes = jnp.sum(hold[:, cut:].astype(jnp.float32), axis=0)
            raised = jnp.where(numbers(NOTES) == 1, jnp.minimum(notes, 1.0), 0.0)
            relay = relay + jnp.pad(raised, (cut, 0))[None, :]
        relay = relay.astype(jnp.bfloat16)
        arrived = [relay[:step]]
        for b in range(1, NEAR):
            arrived.append(moved(relay[b * step : (b + 1) * step], chip_step=b))
        previous = arrived[1:]
        if h:
            arrived, products = lax.optimization_barrier((arrived, products))
        given = jnp.concatenate([p[side:] for p in arrived] + [over[h][SLOTS:]], axis=0)
        kept = jnp.concatenate([p[:side] for p in arrived] + [over[h][:SLOTS]], axis=0)
        got = moved(given, flip=True)
        if h == 0:
            seen = jnp.maximum(jnp.max(kept[:, cut + 1]), jnp.max(got[:, cut + 1]))
        met = jnp.concatenate([kept[:, :cut], got[:, :cut]], axis=0)
        dims = (((1,), (1,)), ((), ()))
        products += lax.dot_general(
            met, weight[:, share], dims, preferred_element_type=jnp.float32
        )
    products = products.astype(jnp.bfloat16)

    part = products.shape[0] // 2
    stay = products[:part]
    gone = moved(products[part:], flip=True)
    pieces = []
    for b in range(NEAR):
        cell = slice(b * side, (b + 1) * side)
        piece = jnp.concatenate([stay[cell], gone[cell]], axis=0)
        pieces.append(moved(piece, chip_step=-b) if b else piece)
    piece = jnp.concatenate([stay[NEAR * side :], gone[NEAR * side :]], axis=0)
    over_back = moved(piece, chip_step=-half)
    relayed = picked(relay_pick.T, jnp.concatenate(pieces, axis=0))
    final = [relayed[:BLOCK]]
    for a in range(1, blocks):
        piece = relayed[BLOCK + (a - 1) * PACKED : BLOCK + a * PACKED]
        final.append(moved(piece, chip_step=-a * NEAR))
    final = jnp.concatenate(final + [over_back], axis=0)
    own = picked(send_pick[:, :tokens].T, final)
    other = picked(send_pick[:, tokens:].T, final)
    return own + moved(other, flip=True), seen


def local(cotangent, expert_ids, route_weight, saved_preact, down_weight):
    weight = down_weight[0]
    width = weight.shape[0]
    far_rows = moved(cotangent, flip=True)
    expert = moved(expert_ids[:, 0], section_step=1)
    far_expert = moved(expert_ids[:, 0], section_step=1, flip=True)
    rank = ranked(expert)
    result, full = packed(cotangent, far_rows, expert, far_expert, rank, weight)
    result = lax.cond(
        full > 0,
        lambda: direct(cotangent, expert, rank, weight),
        lambda: result,
    )

    sections = lax.axis_size("section")
    route = [((i + 1) % sections, i) for i in range(sections)]
    back_hidden = lax.ppermute(result, "section", route)
    gate_value = saved_preact[:, :width].astype(jnp.float32)
    up_value = saved_preact[:, width:].astype(jnp.float32)
    sigmoid_gate = jax.nn.sigmoid(gate_value)
    activated = gate_value * sigmoid_gate
    hidden = activated * up_value
    result_float = back_hidden.astype(jnp.float32)
    d_route = jnp.sum(result_float * hidden, axis=1)
    grad_hidden = route_weight[:, None] * result_float
    d_gate = grad_hidden * up_value * sigmoid_gate * (1.0 + gate_value * (1.0 - sigmoid_gate))
    d_up = grad_hidden * activated
    d_preact = jnp.concatenate([d_gate, d_up], axis=1).astype(jnp.bfloat16)
    return (d_preact, d_route)


def solution(mesh):
    in_specs = (
        P(("section", "expert"), None),
        P(("section", "expert"), None),
        P(("section", "expert")),
        P(("section", "expert"), None),
        P("expert", None, None),
    )
    out_specs = (P(("section", "expert"), None), P(("section", "expert")))
    return jax.shard_map(local, mesh=mesh, in_specs=in_specs, out_specs=out_specs, check_vma=False)
```
